32 devices in a mesh: sec: 4 (over z), blk: 8 (over y, x, core).
Axes of the slice: x: 2, y: 2, z: 4, core: 2. Of those that a mesh axis runs over, the one named last changes fastest.
Arguments:
- raw: bfloat16 [32, 128, 256], P(('sec', 'blk')), may hold values from -6 to 6
- tissue: int32 [4, 8, 4], P('sec', 'blk'), may hold values 0 or 1
- w_emb: bfloat16 [32, 3, 3], replicated, may hold values from -3 to 3
- w_one: bfloat16 [32, 32, 3, 3], replicated, may hold values from -0.5 to 0.5
- w_down: bfloat16 [64, 32, 2, 2], replicated, may hold values from -0.75 to 0.75
- w_deep: bfloat16 [64, 64, 3, 3, 3], replicated, may hold values from -0.21875 to 0.21875
- w_up: bfloat16 [32, 64, 2, 2], replicated, may hold values from -1 to 1
- w_out: bfloat16 [3, 32], replicated, may hold values from -1 to 1
Outputs:
- logits: float32 [3, 32, 128, 256], P(None, 'sec', 'blk')
The draws below stay inside these ranges and needn't reach their ends.
Inputs may be any that keep to these rules, and one draw needn't show every extreme that they name: 1 marks a block of 8 sections, 16 columns and one 4-th of the rows that holds tissue, 0 one without.
All inputs are finite; a program needn't handle non-finite values.
Results may differ from the reference program's by a relative error of at most 0.0067.
Values may be sent and summed in bfloat16 or wider, within the bound.
A program may use at most 256 MiB of HBM per device.

```python
import jax
import jax.numpy as jnp
from jax import lax

C1 = 32
C2 = 64
YB = 4
XD = 16
SY = 256
ZB = 8
Z = 32
SX = 128
ZSLABS = 4
STRIPES = 8


def place_ends(result, key, low, top_value):
    longest = result.shape.index(max(result.shape))
    spots = []
    for shift in (0, 1):
        where = [jax.random.randint(jax.random.fold_in(key, axis), (), 0, length) for axis, length in enumerate(result.shape)]
        where[longest] = (where[longest] + shift) % result.shape[longest]
        spots.append(tuple(where))
    return result.at[spots[0]].set(low).at[spots[1]].set(top_value)


def block_levels(own_key, dims, split, smallest, largest):
    gain, own = 1.0, jax.random.fold_in(own_key, 6)
    for axis_at, shards_of in split:
        steps = jnp.exp(jax.random.uniform(jax.random.fold_in(own, axis_at), (shards_of,), jnp.float32, smallest / len(split), largest / len(split)))
        gain = gain * jnp.repeat(steps, dims[axis_at] // shards_of).reshape([-1 if axis == axis_at else 1 for axis in range(len(dims))])
    return gain


def normal_values(key, dims, width, most, cuts=(), kind=jnp.bfloat16):
    values = jax.random.normal(key, dims, jnp.float32) * width
    if len(cuts) > 0:
        values = block_levels(key, dims, cuts, -0.22, 0.18) * values
    return jnp.clip(values, min=-most, max=most).astype(kind)


def setup_inputs(seed: int = 0) -> dict:
    streams_of = jax.random.split(jax.random.key(seed), 9)
    raw = normal_values(streams_of[0], (Z, SX, SY), 1.0, 6.0, ((0, 32),))
    tissue = place_ends((jax.random.randint(streams_of[1], (ZSLABS, STRIPES, YB), 0, 2) < 1).astype(jnp.int32), jax.random.fold_in(streams_of[1], 1), 0, 1)
    w_emb = normal_values(streams_of[2], (C1, 3, 3), 4 ** -0.5, 3.0)
    w_one = normal_values(streams_of[3], (C1, C1, 3, 3), (9 * C1 // 2) ** -0.5, 0.5)
    w_down = normal_values(streams_of[4], (C2, C1, 2, 2), (2 * C1) ** -0.5, 0.75)
    w_deep = normal_values(streams_of[5], (C2, C2, 3, 3, 3), (27 * C2 // 2) ** -0.5, 0.21875)
    w_up = normal_values(streams_of[6], (C1, C2, 2, 2), (C2 // 2) ** -0.5, 1.0)
    w_out = normal_values(streams_of[7], (3, C1), C1 ** -0.5, 1.0)
    return {"raw": raw, "tissue": tissue, "w_emb": w_emb, "w_one": w_one, "w_down": w_down, "w_deep": w_deep, "w_up": w_up, "w_out": w_out}


highest = lax.Precision.HIGHEST


def convolve(inputs, kernel, strides, padding, numbers):
    return lax.conv_general_dilated(inputs, kernel, strides, padding, dimension_numbers=numbers, precision=highest)


def level_one(section_plane, mask_plane, w_emb, w_one, w_down):
    masked = section_plane.astype(jnp.float32) * mask_plane
    planar = ("NCHW", "OIHW", "NCHW")
    embedded = convolve(masked[None, None], w_emb.astype(jnp.float32)[:, None], (1, 1), [(1, 1), (1, 1)], planar)
    embedded = jnp.maximum(embedded, 0.0).astype(jnp.bfloat16)
    first_sum = convolve(embedded.astype(jnp.float32), w_one.astype(jnp.float32), (1, 1), [(1, 1), (1, 1)], planar)
    features = (jnp.maximum(first_sum, 0.0) * mask_plane).astype(jnp.bfloat16)
    lowered = convolve(features.astype(jnp.float32), w_down.astype(jnp.float32), (2, 2), [(0, 0), (0, 0)], planar)
    down = (jnp.maximum(lowered, 0.0) * mask_plane[::2, ::2]).astype(jnp.bfloat16)
    return features[0], down[0]


def reference(raw, tissue, w_emb, w_one, w_down, w_deep, w_up, w_out):
    span_y = SY // YB
    mask_cells = jnp.repeat(jnp.repeat(jnp.repeat(tissue.astype(jnp.float32), ZB, 0), XD, 1), span_y, 2)

    def first_pass(pieces):
        return level_one(pieces[0], pieces[1], w_emb, w_one, w_down)[1]

    downs = lax.map(first_pass, (raw, mask_cells))
    padded = jnp.pad(downs, ((1, 1), (0, 0), (0, 0), (0, 0)))

    def second_pass(position):
        section_plane = lax.dynamic_index_in_dim(raw, position, 0, keepdims=False)
        mask_plane = lax.dynamic_index_in_dim(mask_cells, position, 0, keepdims=False)
        features, unused = level_one(section_plane, mask_plane, w_emb, w_one, w_down)
        z_window = lax.dynamic_slice_in_dim(padded, position, 3, 0)
        z_window = jnp.transpose(z_window, (1, 0, 2, 3))[None].astype(jnp.float32)
        deep_sum = convolve(z_window, w_deep.astype(jnp.float32), (1, 1, 1), [(0, 0), (1, 1), (1, 1)], ("NCDHW", "OIDHW", "NCDHW"))
        deep = (jnp.maximum(deep_sum[0, :, 0], 0.0) * mask_plane[::2, ::2]).astype(jnp.bfloat16)
        raised = jnp.einsum("ocab,cxy->oxayb", w_up.astype(jnp.float32), deep.astype(jnp.float32), precision=highest)
        raised = raised.reshape(C1, SX, SY)
        decoded = (jnp.maximum(raised + features.astype(jnp.float32), 0.0) * mask_plane).astype(jnp.bfloat16)
        projected = jnp.einsum("oc,cxy->oxy", w_out.astype(jnp.float32), decoded.astype(jnp.float32), precision=highest)
        return projected * mask_plane

    planes = lax.map(second_pass, jnp.arange(Z, dtype=jnp.int32))
    return jnp.transpose(planes, (1, 0, 2, 3))
```

```python
import functools

import jax
import jax.numpy as jnp
from jax import lax
from jax.experimental import pallas as pl
from jax.experimental.pallas import tpu as pltpu
from jax.sharding import PartitionSpec as P

F32 = jnp.float32
BF16 = jnp.bfloat16
MESH = pl.DeviceIdType.MESH
NT = (((1,), (1,)), ((), ()))


def exchange_kernel(
    ns, nb, raw_ref, tissue_ref, recv_ref, masks_ref, stage, mine, send_sem, recv_sem, up_sem,
    mask_send, mask_recv, local_sem
):
    sec = lax.axis_index("sec")
    blk = lax.axis_index("blk")
    has_below = sec > 0
    has_above = sec < ns - 1

    barrier = pltpu.get_barrier_semaphore()
    for k in range(1, nb):
        pl.semaphore_signal(
            barrier, inc=1, device_id=(sec, lax.rem(blk + k, nb)), device_id_type=MESH
        )

    @pl.when(has_below)
    def _():
        for k in range(nb):
            pl.semaphore_signal(barrier, inc=1, device_id=(sec - 1, k), device_id_type=MESH)

    @pl.when(has_above)
    def _():
        for k in range(nb):
            pl.semaphore_signal(barrier, inc=1, device_id=(sec + 1, k), device_id_type=MESH)

    section = raw_ref[0].astype(F32)
    nothing = jnp.zeros((8, section.shape[1]), F32)
    for k in range(nb):
        low, high = max(16 * k - 4, 0), min(16 * k + 20, 16 * nb)
        parts = [section[low:high], nothing]
        if k == 0:
            parts = [nothing[:4]] + parts
        if k == nb - 1:
            parts = parts + [nothing[:4]]
        stage[k] = jnp.concatenate(parts, axis=0).astype(BF16)
    for row in range(4):
        value = tissue_ref[0, 0, row].astype(F32)
        mine[row : row + 1, :] = jnp.full((1, 128), value, F32)
    mine[4:8, :] = jnp.zeros((4, 128), F32)
    masks_ref[4] = mine[...]

    @pl.when(jnp.logical_not(has_below))
    def _():
        recv_ref[0] = jnp.zeros(recv_ref.shape[1:], BF16)

    @pl.when(jnp.logical_not(has_above))
    def _():
        recv_ref[nb + 1] = jnp.zeros(recv_ref.shape[1:], BF16)

    local = pltpu.make_async_copy(stage.at[blk], recv_ref.at[blk + 1], local_sem)
    local.start()

    count = (nb - 1) + nb * has_below.astype(jnp.int32) + nb * has_above.astype(jnp.int32)
    pl.semaphore_wait(barrier, count)

    send_up = jnp.logical_and(has_above, blk == nb - 1)
    send_down = jnp.logical_and(has_below, blk == 0)

    def outer(target, slot, sem, k):
        return pltpu.make_async_remote_copy(
            src_ref=stage.at[k],
            dst_ref=recv_ref.at[slot],
            send_sem=up_sem.at[k],
            recv_sem=recv_sem.at[sem],
            device_id=(target, k),
            device_id_type=MESH,
        )

    @pl.when(send_up)
    def _():
        for k in range(nb):
            outer(sec + 1, 0, nb, k).start()

    @pl.when(send_down)
    def _():
        for k in range(nb):
            outer(sec - 1, nb + 1, nb + 1, k).start()

    copies = []
    for k in range(1, nb):
        target = lax.rem(blk + k, nb)
        copy = pltpu.make_async_remote_copy(
            src_ref=stage.at[target],
            dst_ref=recv_ref.at[blk + 1],
            send_sem=send_sem.at[k],
            recv_sem=recv_sem.at[k],
            device_id=(sec, target),
            device_id_type=MESH,
        )
        copy.start()
        copies.append(copy)

    def present(es, eb):
        ok = None
        for at, step, count_of in ((sec, es, ns), (blk, eb, nb)):
            if step == 0:
                continue
            term = at > 0 if step < 0 else at < count_of - 1
            ok = term if ok is None else jnp.logical_and(ok, term)
        return ok

    def mask_copy(es, eb):
        slot = (1 - es) * 3 + (1 - eb)
        return pltpu.make_async_remote_copy(
            src_ref=mine,
            dst_ref=masks_ref.at[slot],
            send_sem=mask_send.at[slot],
            recv_sem=mask_recv.at[slot],
            device_id=(sec + es, blk + eb),
            device_id_type=MESH,
        )

    around = [(es, eb) for es in (-1, 0, 1) for eb in (-1, 0, 1) if (es, eb) != (0, 0)]
    for es, eb in around:

        @pl.when(present(es, eb))
        def _(es=es, eb=eb):
            mask_copy(es, eb).start()

        @pl.when(jnp.logical_not(present(es, eb)))
        def _(es=es, eb=eb):
            masks_ref[(1 + es) * 3 + (1 + eb)] = jnp.zeros((8, 128), F32)

    for es, eb in around:

        @pl.when(present(es, eb))
        def _(es=es, eb=eb):
            mask_copy(es, eb).wait_send()
            mask_copy(-es, -eb).wait_recv()

    local.wait()
    for copy in copies:
        copy.wait_send()
        copy.wait_recv()

    @pl.when(send_up)
    def _():
        for k in range(nb):
            outer(sec + 1, 0, nb, k).wait_send()

    @pl.when(send_down)
    def _():
        for k in range(nb):
            outer(sec - 1, nb + 1, nb + 1, k).wait_send()

    @pl.when(has_below)
    def _():
        outer(sec - 1, 0, nb, 0).wait_recv()

    @pl.when(has_above)
    def _():
        outer(sec + 1, nb + 1, nb + 1, 0).wait_recv()


def exchange(raw, tissue, ns, nb):
    length_y = raw.shape[2]
    return pl.pallas_call(
        functools.partial(exchange_kernel, ns, nb),
        out_shape=(
            jax.ShapeDtypeStruct((nb + 2, 32, length_y), BF16),
            jax.ShapeDtypeStruct((9, 8, 128), F32),
        ),
        in_specs=[
            pl.BlockSpec(memory_space=pltpu.VMEM),
            pl.BlockSpec(memory_space=pltpu.SMEM),
        ],
        out_specs=(pl.BlockSpec(memory_space=pltpu.VMEM), pl.BlockSpec(memory_space=pltpu.VMEM)),
        scratch_shapes=[
            pltpu.VMEM((nb, 32, length_y), BF16),
            pltpu.VMEM((8, 128), F32),
            pltpu.SemaphoreType.DMA((nb,)),
            pltpu.SemaphoreType.DMA((nb + 2,)),
            pltpu.SemaphoreType.DMA((nb,)),
            pltpu.SemaphoreType.DMA((9,)),
            pltpu.SemaphoreType.DMA((9,)),
            pltpu.SemaphoreType.DMA,
        ],
        compiler_params=pltpu.CompilerParams(collective_id=0, has_side_effects=True),
        name="exchange",
    )(raw, tissue)


def iota(shape, dim):
    return lax.broadcasted_iota(jnp.int32, shape, dim)


def dot(a, b):
    return jnp.dot(a, b, preferred_element_type=F32)


def network_kernel(
    nb, recv_ref, masks_ref, emb_ref, one_ref, down_ref, deep_ref, up_ref, out_w_ref, blk_ref,
    logits_ref, perm4, perm_out, w_e, w_c, w_h, w_d0, w_d1, w_d2, w_z, w_u, w_o, deep_t, one_t,
    planes, feats, tall, downs, decoded
):
    nz = nb
    lane = iota((1, 128), 1)

    def put(dst, row, rows, tile, size, blocks):
        total = None
        for q, block in enumerate(blocks):
            if block is None:
                continue
            if total is None:
                total = jnp.where(lane // size == q, block(), 0.0)
            else:
                total = jnp.where(lane // size == q, block(), total)
        if total is None:
            total = jnp.zeros((rows, 128), F32)
        dst[row : row + rows, 128 * tile : 128 * tile + 128] = total.astype(BF16)

    y_of = iota((512, 256), 0)
    perm4[...] = jnp.where(
        iota((512, 256), 1) == 2 * (y_of % 128) - 1 + y_of // 128, 1.0, 0.0
    ).astype(BF16)
    row_of = iota((256, 256), 0)
    perm_out[...] = jnp.where(
        iota((256, 256), 1) == 2 * (row_of % 128) + row_of // 128, 1.0, 0.0
    ).astype(BF16)

    first_x = 16 * blk_ref[0]
    for tile in range(6):
        x_of = lane // 32 + (4 * tile - 1 if tile < 5 else -3)
        inside = jnp.logical_and(x_of + first_x >= 0, x_of + first_x < 16 * nb)
        for b in range(3):
            total = jnp.zeros((32, 128), F32)
            for a in range(3):
                weight = emb_ref[a * 3 + b : a * 3 + b + 1, :].astype(F32)
                hit = jnp.logical_and(iota((32, 128), 0) == x_of + a + 3, inside)
                total = jnp.where(hit, weight, total)
            w_e[32 * b : 32 * b + 32, 128 * tile : 128 * tile + 128] = total.astype(BF16)
    w_e[96:128, :] = jnp.zeros((32, 768), BF16)

    eye = jnp.where(iota((64, 64), 0) == iota((64, 64), 1), 1.0, 0.0).astype(BF16)
    eye32 = jnp.where(iota((32, 32), 0) == iota((32, 32), 1), 1.0, 0.0).astype(BF16)
    for s in range(3):
        for a in range(3):
            for b in range(3):
                block = deep_ref[s, a, b]
                deep_t[(s * 3 + b) * 3 + a] = lax.dot_general(
                    eye, jnp.concatenate([block, block], axis=0), NT, preferred_element_type=F32
                )
    for a in range(3):
        for b in range(3):
            block = one_ref[a, b]
            one_t[b * 3 + a] = lax.dot_general(
                eye32, jnp.concatenate([block] * 4, axis=0), NT, preferred_element_type=F32
            )

    def one_block(b, a):
        return (lambda: one_t[b * 3 + a]) if 0 <= a <= 2 else None

    for b in range(3):
        for e in range(12):
            for tile in range(2):
                blocks = [one_block(b, e - 4 * tile - q) for q in range(4)]
                put(w_c, (b * 12 + e) * 32, 32, tile, 32, blocks)
        for e in range(4):
            pair = [one_block(b, e), one_block(b, e - 1)]
            put(w_h, (b * 8 + e) * 32, 32, 0, 32, [None, None] + pair)
            put(w_h, (b * 8 + 4 + e) * 32, 32, 0, 32, pair + [None, None])

    def down_block(p, x, half):
        a = x - 2 * half
        return (lambda: down_ref[p * 2 + a].astype(F32)) if 0 <= a <= 1 else None

    rims = [-2, -1, 16, 17]
    for dst, columns, halves in (
        (w_d0, list(range(8)) + rims, [-1, 0, 1, 2]),
        (w_d1, list(range(4, 16)), [3, 4, 5, 6]),
        (w_d2, list(range(12, 16)) + rims, [7, 8]),
    ):
        for p in range(2):
            for at, x in enumerate(columns):
                for tile in range(len(halves) // 2):
                    blocks = [down_block(p, x, halves[2 * tile + q]) for q in range(2)]
                    put(dst, (p * len(columns) + at) * 32, 32, tile, 64, blocks)

    def deep_block(s, b, a):
        return (lambda: deep_t[(s * 3 + b) * 3 + a]) if 0 <= a <= 2 else None

    for s in range(3):
        for b in range(3):
            for e in range(6):
                for tile in range(2):
                    blocks = [deep_block(s, b, e - 2 * tile - q) for q in range(2)]
                    put(w_z, ((s * 3 + b) * 6 + e) * 64, 64, tile, 64, blocks)

    for p in range(2):
        block = up_ref[p]
        turned = lax.dot_general(
            eye, jnp.concatenate([block, block], axis=0), NT, preferred_element_type=F32
        )
        for i in range(4):
            for tile in range(2):
                blocks = [(lambda: turned) if i == 2 * tile + q else None for q in range(2)]
                put(w_u, i * 64, 64, p * 2 + tile, 64, blocks)

    for tile in range(4):
        for d in range(3):
            weight = out_w_ref[d : d + 1, :].astype(F32)
            w_o[16 * d : 16 * d + 16, 128 * tile : 128 * tile + 128] = jnp.where(
                iota((16, 128), 0) == lane // 32 + 4 * tile, weight, 0.0
            ).astype(BF16)

    for u in range(2):
        tall[u, 0:8, :] = jnp.zeros((8, 640), F32)
        tall[u, 136:144, :] = jnp.zeros((8, 640), F32)

    @pl.loop(0, (nz + 2) // 2)
    def _(step):
        marks = []
        shifted = []
        for u in range(2):
            z = 2 * step + u
            zone = jnp.where(z == 0, 0, jnp.where(z == nz + 1, 2, 1))
            three = [masks_ref[zone * 3 + k] for k in range(3)]
            marks.append(three)

            def along(m):
                return jnp.concatenate(
                    [
                        jnp.where(lane < 64, m[0:1], m[1:2]),
                        jnp.where(lane < 64, m[2:3], m[3:4]),
                    ],
                    axis=1,
                )

            row = iota((32, 256), 0)
            mask = jnp.where(row < 4, along(three[0]), jnp.where(row < 20, along(three[1]), along(three[2])))
            masked = recv_ref[z].astype(F32) * mask
            column = iota((32, 256), 1)
            before = jnp.where(column == 0, 0.0, pltpu.roll(masked, 1, 1))
            after = jnp.where(column == 255, 0.0, pltpu.roll(masked, 255, 1))
            shifted += [before, masked, after, jnp.zeros((32, 256), F32)]
        shifted = jnp.concatenate(shifted, axis=0).astype(BF16)
        turned = lax.dot_general(perm4[...], shifted, NT, preferred_element_type=F32).astype(BF16)
        for u in range(2):
            embedded = dot(turned[:, 128 * u : 128 * u + 128], w_e[...])
            planes[u] = jnp.maximum(embedded, 0.0).astype(BF16)

        def windows(low, high):
            return jnp.concatenate(
                [
                    jnp.concatenate(
                        [planes[u, 128 * (p + b) : 128 * (p + b) + 128, low:high] for b in range(3)],
                        axis=1,
                    )
                    for u in range(2)
                    for p in range(2)
                ],
                axis=0,
            )

        def keep(summed, first, width, marks_of):
            for u in range(2):
                z = 2 * step + u
                rows_of = marks_of(marks[u])
                for p in range(2):
                    for y in range(4):
                        at = 128 * p + 32 * y
                        piece = summed[256 * u + at : 256 * u + at + 32]
                        piece = jnp.maximum(piece, 0.0) * rows_of[y]
                        feats[z, at : at + 32, first : first + width] = piece.astype(BF16)

        def inner(three):
            return [jnp.concatenate([three[1][y : y + 1]] * 2, axis=1) for y in range(4)]

        def outer(three):
            return [jnp.where(lane < 64, three[0][y : y + 1], three[2][y : y + 1]) for y in range(4)]

        keep(dot(windows(0, 384), w_c[...]), 0, 256, inner)
        keep(dot(windows(256, 640), w_c[...]), 256, 256, inner)
        keep(dot(windows(512, 768), w_h[...]), 512, 128, outer)

        def pairs(spans):
            return jnp.concatenate(
                [
                    jnp.concatenate(
                        [
                            feats[2 * step + u, 128 * p : 128 * p + 128, low:high]
                            for p in range(2)
                            for low, high in spans
                        ],
                        axis=1,
                    )
                    for u in range(2)
                ],
                axis=0,
            )

        lowered = [
            dot(pairs([(0, 256), (512, 640)]), w_d0[...]),
            dot(pairs([(128, 512)]), w_d1[...]),
            dot(pairs([(384, 640)]), w_d2[...]),
        ]
        for u in range(2):
            left, middle, right = marks[u]
            for y in range(4):
                m = middle[y : y + 1]
                rows_of = [
                    jnp.concatenate([jnp.where(lane < 64, left[y : y + 1], m), m], axis=1),
                    jnp.concatenate([m, m], axis=1),
                    jnp.where(lane < 64, m, right[y : y + 1]),
                ]
                for part, width in ((0, 256), (1, 256), (2, 128)):
                    piece = lowered[part][128 * u + 32 * y : 128 * u + 32 * y + 32]
                    piece = jnp.maximum(piece, 0.0) * rows_of[part]
                    tall[u, 8 + 32 * y : 40 + 32 * y, 256 * part : 256 * part + width] = piece
            for b in range(3):
                downs[2 * step + u, b] = tall[u, 7 + b : 135 + b, :].astype(BF16)

    @pl.loop(0, nz // 2)
    def _(step):
        middle = masks_ref[4]
        rows_of = [jnp.concatenate([middle[y : y + 1]] * 2, axis=1) for y in range(4)]
        gathered = jnp.concatenate(
            [
                jnp.concatenate(
                    [
                        downs[2 * step + u + s, b, :, 256 * g : 256 * g + 384]
                        for s in range(3)
                        for b in range(3)
                    ],
                    axis=1,
                )
                for g in range(2)
                for u in range(2)
            ],
            axis=0,
        )
        deep_sum = dot(gathered, w_z[...])
        deep = jnp.concatenate(
            [
                jnp.maximum(deep_sum[32 * r : 32 * r + 32], 0.0) * rows_of[r % 4]
                for r in range(16)
            ],
            axis=0,
        ).astype(BF16)
        raised = dot(deep, w_u[...])
        for g in range(2):
            for u in range(2):
                for p in range(2):
                    for y in range(4):
                        at = 128 * p + 32 * y
                        row = 256 * g + 128 * u + 32 * y
                        piece = raised[row : row + 32, 256 * p : 256 * p + 256]
                        skip = feats[2 * step + u + 1, at : at + 32, 256 * g : 256 * g + 256]
                        piece = jnp.maximum(piece + skip.astype(F32), 0.0) * rows_of[y]
                        decoded[u, at : at + 32, 256 * g : 256 * g + 256] = piece.astype(BF16)
        halves = []
        for u in range(2):
            projected = lax.dot_general(w_o[...], decoded[u], NT, preferred_element_type=F32)
            high = projected.astype(BF16)
            halves += [high, (projected - high.astype(F32)).astype(BF16)]
        ordered = dot(jnp.concatenate(halves, axis=0), perm_out[...])
        y_mask = jnp.concatenate(
            [
                jnp.where(lane < 64, middle[0:1], middle[1:2]),
                jnp.where(lane < 64, middle[2:3], middle[3:4]),
            ],
            axis=1,
        )
        for u in range(2):
            both = (ordered[96 * u : 96 * u + 48] + ordered[96 * u + 48 : 96 * u + 96]) * y_mask
            for d in range(3):
                logits_ref[d, 2 * step + u] = both[16 * d : 16 * d + 16]


def network(recv, masks, w_emb, w_one, w_down, w_deep, w_up, w_out, blk, nb, interpret=False):
    nz, length_y = nb, recv.shape[2]
    emb = jnp.tile(jnp.transpose(w_emb, (1, 2, 0)).reshape(9, 32), (1, 4))
    one = jnp.transpose(w_one, (2, 3, 0, 1))
    down = jnp.tile(jnp.transpose(w_down, (3, 2, 1, 0)).reshape(4, 32, 64), (1, 1, 2))
    deep = jnp.transpose(w_deep, (2, 3, 4, 0, 1))
    up = jnp.transpose(w_up, (3, 2, 0, 1)).reshape(2, 64, 64)
    out_w = jnp.tile(w_out, (1, 4))
    return pl.pallas_call(
        functools.partial(network_kernel, nb),
        out_shape=jax.ShapeDtypeStruct((3, nz, 16, length_y), F32),
        in_specs=[pl.BlockSpec(memory_space=pltpu.VMEM)] * 8
        + [pl.BlockSpec(memory_space=pltpu.SMEM)],
        out_specs=pl.BlockSpec(memory_space=pltpu.VMEM),
        scratch_shapes=[
            pltpu.VMEM((512, 256), BF16),
            pltpu.VMEM((256, 256), BF16),
            pltpu.VMEM((128, 768), BF16),
            pltpu.VMEM((1152, 256), BF16),
            pltpu.VMEM((768, 128), BF16),
            pltpu.VMEM((768, 256), BF16),
            pltpu.VMEM((768, 256), BF16),
            pltpu.VMEM((512, 128), BF16),
            pltpu.VMEM((3456, 256), BF16),
            pltpu.VMEM((256, 512), BF16),
            pltpu.VMEM((48, 512), BF16),
            pltpu.VMEM((27, 64, 128), F32),
            pltpu.VMEM((9, 32, 128), F32),
            pltpu.VMEM((2, 512, 768), BF16),
            pltpu.VMEM((nz + 2, 256, 640), BF16),
            pltpu.VMEM((2, 144, 640), F32),
            pltpu.VMEM((nz + 2, 3, 128, 640), BF16),
            pltpu.VMEM((2, 256, 512), BF16),
        ],
        compiler_params=pltpu.CompilerParams(vmem_limit_bytes=56 * 1024 * 1024),
        name="network",
        interpret=interpret,
    )(recv, masks, emb, one, down, deep, up, out_w, blk)


def solution(mesh):
    ns, nb = mesh.shape["sec"], mesh.shape["blk"]

    def per_device(raw, tissue, *weights):
        recv, masks = exchange(raw, tissue, ns, nb)
        blk = jnp.full((1,), lax.axis_index("blk"), jnp.int32)
        return network(recv, masks, *weights, blk, nb)

    placed = (P(("sec", "blk"), None, None), P("sec", "blk", None), P(), P(), P(), P(), P(), P())
    return jax.shard_map(
        per_device,
        mesh=mesh,
        in_specs=placed,
        out_specs=P(None, "sec", "blk", None),
        check_vma=False,
    )
```

```python
import functools

import jax
import jax.numpy as jnp
from jax import lax
from jax.experimental import pallas as pl
from jax.experimental.pallas import tpu as pltpu
from jax.sharding import PartitionSpec as P

F32 = jnp.float32
BF16 = jnp.bfloat16
MESH = pl.DeviceIdType.MESH
NT = (((1,), (1,)), ((), ()))


def exchange_kernel(
    ns, nb, raw_ref, tissue_ref, recv_ref, masks_ref, stage, mine, send_sem, recv_sem, up_sem,
    mask_send, mask_recv, local_sem
):
    sec = lax.axis_index("sec")
    blk = lax.axis_index("blk")
    has_below = sec > 0
    has_above = sec < ns - 1

    barrier = pltpu.get_barrier_semaphore()
    for k in range(1, nb):
        pl.semaphore_signal(
            barrier, inc=1, device_id=(sec, lax.rem(blk + k, nb)), device_id_type=MESH
        )

    @pl.when(has_below)
    def _():
        for k in range(nb):
            pl.semaphore_signal(barrier, inc=1, device_id=(sec - 1, k), device_id_type=MESH)

    @pl.when(has_above)
    def _():
        for k in range(nb):
            pl.semaphore_signal(barrier, inc=1, device_id=(sec + 1, k), device_id_type=MESH)

    section = raw_ref[0].astype(F32)
    nothing = jnp.zeros((8, section.shape[1]), F32)
    for k in range(nb):
        low, high = max(16 * k - 4, 0), min(16 * k + 20, 16 * nb)
        parts = [section[low:high], nothing]
        if k == 0:
            parts = [nothing[:4]] + parts
        if k == nb - 1:
            parts = parts + [nothing[:4]]
        stage[k] = jnp.concatenate(parts, axis=0).astype(BF16)
    for row in range(4):
        value = tissue_ref[0, 0, row].astype(F32)
        mine[row : row + 1, :] = jnp.full((1, 128), value, F32)
    mine[4:8, :] = jnp.zeros((4, 128), F32)
    masks_ref[4] = mine[...]

    @pl.when(jnp.logical_not(has_below))
    def _():
        recv_ref[0] = jnp.zeros(recv_ref.shape[1:], BF16)

    @pl.when(jnp.logical_not(has_above))
    def _():
        recv_ref[nb + 1] = jnp.zeros(recv_ref.shape[1:], BF16)

    local = pltpu.make_async_copy(stage.at[blk], recv_ref.at[blk + 1], local_sem)
    local.start()

    count = (nb - 1) + nb * has_below.astype(jnp.int32) + nb * has_above.astype(jnp.int32)
    pl.semaphore_wait(barrier, count)

    send_up = jnp.logical_and(has_above, blk == nb - 1)
    send_down = jnp.logical_and(has_below, blk == 0)

    def outer(target, slot, sem, k):
        return pltpu.make_async_remote_copy(
            src_ref=stage.at[k],
            dst_ref=recv_ref.at[slot],
            send_sem=up_sem.at[k],
            recv_sem=recv_sem.at[sem],
            device_id=(target, k),
            device_id_type=MESH,
        )

    @pl.when(send_up)
    def _():
        for k in range(nb):
            outer(sec + 1, 0, nb, k).start()

    @pl.when(send_down)
    def _():
        for k in range(nb):
            outer(sec - 1, nb + 1, nb + 1, k).start()

    copies = []
    for k in range(1, nb):
        target = lax.rem(blk + k, nb)
        copy = pltpu.make_async_remote_copy(
            src_ref=stage.at[target],
            dst_ref=recv_ref.at[blk + 1],
            send_sem=send_sem.at[k],
            recv_sem=recv_sem.at[k],
            device_id=(sec, target),
            device_id_type=MESH,
        )
        copy.start()
        copies.append(copy)

    def present(es, eb):
        ok = None
        for at, step, count_of in ((sec, es, ns), (blk, eb, nb)):
            if step == 0:
                continue
            term = at > 0 if step < 0 else at < count_of - 1
            ok = term if ok is None else jnp.logical_and(ok, term)
        return ok

    def mask_copy(es, eb):
        slot = (1 - es) * 3 + (1 - eb)
        return pltpu.make_async_remote_copy(
            src_ref=mine,
            dst_ref=masks_ref.at[slot],
            send_sem=mask_send.at[slot],
            recv_sem=mask_recv.at[slot],
            device_id=(sec + es, blk + eb),
            device_id_type=MESH,
        )

    around = [(es, eb) for es in (-1, 0, 1) for eb in (-1, 0, 1) if (es, eb) != (0, 0)]
    for es, eb in around:

        @pl.when(present(es, eb))
        def _(es=es, eb=eb):
            mask_copy(es, eb).start()

        @pl.when(jnp.logical_not(present(es, eb)))
        def _(es=es, eb=eb):
            masks_ref[(1 + es) * 3 + (1 + eb)] = jnp.zeros((8, 128), F32)

    for es, eb in around:

        @pl.when(present(es, eb))
        def _(es=es, eb=eb):
            mask_copy(es, eb).wait_send()
            mask_copy(-es, -eb).wait_recv()

    local.wait()
    for copy in copies:
        copy.wait_send()
        copy.wait_recv()

    @pl.when(send_up)
    def _():
        for k in range(nb):
            outer(sec + 1, 0, nb, k).wait_send()

    @pl.when(send_down)
    def _():
        for k in range(nb):
            outer(sec - 1, nb + 1, nb + 1, k).wait_send()

    @pl.when(has_below)
    def _():
        outer(sec - 1, 0, nb, 0).wait_recv()

    @pl.when(has_above)
    def _():
        outer(sec + 1, nb + 1, nb + 1, 0).wait_recv()


def exchange(raw, tissue, ns, nb):
    length_y = raw.shape[2]
    return pl.pallas_call(
        functools.partial(exchange_kernel, ns, nb),
        out_shape=(
            jax.ShapeDtypeStruct((nb + 2, 32, length_y), BF16),
            jax.ShapeDtypeStruct((9, 8, 128), F32),
        ),
        in_specs=[
            pl.BlockSpec(memory_space=pltpu.VMEM),
            pl.BlockSpec(memory_space=pltpu.SMEM),
        ],
        out_specs=(pl.BlockSpec(memory_space=pltpu.VMEM), pl.BlockSpec(memory_space=pltpu.VMEM)),
        scratch_shapes=[
            pltpu.VMEM((nb, 32, length_y), BF16),
            pltpu.VMEM((8, 128), F32),
            pltpu.SemaphoreType.DMA((nb,)),
            pltpu.SemaphoreType.DMA((nb + 2,)),
            pltpu.SemaphoreType.DMA((nb,)),
            pltpu.SemaphoreType.DMA((9,)),
            pltpu.SemaphoreType.DMA((9,)),
            pltpu.SemaphoreType.DMA,
        ],
        compiler_params=pltpu.CompilerParams(collective_id=0, has_side_effects=True),
        name="exchange",
    )(raw, tissue)


def iota(shape, dim):
    return lax.broadcasted_iota(jnp.int32, shape, dim)


def dot(a, b):
    return jnp.dot(a, b, preferred_element_type=F32)


def network_kernel(
    nb, recv_ref, masks_ref, emb_ref, one_ref, down_ref, deep_ref, up_ref, out_w_ref, blk_ref,
    logits_ref, perm_out, w_e, w_c, w_h, w_d0, w_d1, w_d2, w_z, w_u, w_o, deep_t, one_t, down_t,
    planes, feats, tall, downs, decoded
):
    nz = nb
    lane = iota((1, 128), 1)

    def put(dst, row, rows, tile, size, blocks):
        total = None
        for q, block in enumerate(blocks):
            if block is None:
                continue
            if total is None:
                total = jnp.where(lane // size == q, block(), 0.0)
            else:
                total = jnp.where(lane // size == q, block(), total)
        if total is None:
            total = jnp.zeros((rows, 128), F32)
        dst[row : row + rows, 128 * tile : 128 * tile + 128] = total.astype(BF16)

    row_of = iota((256, 256), 0)
    perm_out[...] = jnp.where(
        iota((256, 256), 1) == 2 * (row_of % 128) + row_of // 128, 1.0, 0.0
    ).astype(BF16)

    dup32 = jnp.where(iota((32, 128), 0) == iota((32, 128), 1) % 32, 1.0, 0.0).astype(BF16)
    dup64 = jnp.where(iota((64, 128), 0) == iota((64, 128), 1) % 64, 1.0, 0.0).astype(BF16)
    for at in range(4):
        down_t[at] = dot(down_ref[at], dup64)
    emb_rows = [dot(emb_ref[a], dup32) for a in range(3)]
    out_rows = dot(out_w_ref[...], dup32)

    first_x = 16 * blk_ref[0]
    for tile in range(6):
        x_of = lane // 32 + (4 * tile - 1 if tile < 5 else -3)
        inside = jnp.logical_and(x_of + first_x >= 0, x_of + first_x < 16 * nb)
        for b in range(3):
            total = jnp.zeros((32, 128), F32)
            for a in range(3):
                weight = emb_rows[a][b : b + 1, :]
                hit = jnp.logical_and(iota((32, 128), 0) == x_of + a + 3, inside)
                total = jnp.where(hit, weight, total)
            w_e[32 * b : 32 * b + 32, 128 * tile : 128 * tile + 128] = total.astype(BF16)
    w_e[96:128, :] = jnp.zeros((32, 768), BF16)

    eye = jnp.where(iota((64, 64), 0) == iota((64, 64), 1), 1.0, 0.0).astype(BF16)
    eye32 = jnp.where(iota((32, 32), 0) == iota((32, 32), 1), 1.0, 0.0).astype(BF16)
    for s in range(3):
        for a in range(3):
            for b in range(3):
                block = deep_ref[s, a, b]
                deep_t[(s * 3 + b) * 3 + a] = lax.dot_general(
                    eye, jnp.concatenate([block, block], axis=0), NT, preferred_element_type=F32
                )
    for a in range(3):
        for b in range(3):
            block = one_ref[a, b]
            one_t[b * 3 + a] = lax.dot_general(
                eye32, jnp.concatenate([block] * 4, axis=0), NT, preferred_element_type=F32
            )

    def one_block(b, a):
        return (lambda: one_t[b * 3 + a]) if 0 <= a <= 2 and 0 <= b <= 2 else None

    for k in range(4):
        for p in range(2):
            for e in range(8):
                put(w_c, (k * 8 + e) * 32, 32, p, 32, [one_block(k - p, e - q) for q in range(4)])
            for e in range(4):
                pair = [one_block(k - p, e), one_block(k - p, e - 1)]
                put(w_h, (k * 8 + e) * 32, 32, p, 32, [None, None] + pair)
                put(w_h, (k * 8 + 4 + e) * 32, 32, p, 32, pair + [None, None])

    def down_block(p, x, half):
        a = x - 2 * half
        return (lambda: down_t[p * 2 + a]) if 0 <= a <= 1 else None

    rims = [-2, -1, 16, 17]
    for dst, columns, halves in (
        (w_d0, list(range(8)) + rims, [-1, 0, 1, 2]),
        (w_d1, list(range(4, 16)), [3, 4, 5, 6]),
        (w_d2, list(range(12, 16)) + rims, [7, 8]),
    ):
        for p in range(2):
            for at, x in enumerate(columns):
                for tile in range(len(halves) // 2):
                    blocks = [down_block(p, x, halves[2 * tile + q]) for q in range(2)]
                    put(dst, (p * len(columns) + at) * 32, 32, tile, 64, blocks)

    def deep_block(s, b, a):
        return (lambda: deep_t[(s * 3 + b) * 3 + a]) if 0 <= a <= 2 and 0 <= s <= 2 else None

    for k in range(4):
        for b in range(3):
            for e in range(4):
                for tile in range(2):
                    blocks = [deep_block(k - tile, b, e - q) for q in range(2)]
                    put(w_z, ((k * 3 + b) * 4 + e) * 64, 64, tile, 64, blocks)

    for p in range(2):
        block = up_ref[p]
        turned = lax.dot_general(
            eye, jnp.concatenate([block, block], axis=0), NT, preferred_element_type=F32
        )
        for i in range(4):
            for tile in range(2):
                blocks = [(lambda: turned) if i == 2 * tile + q else None for q in range(2)]
                put(w_u, i * 64, 64, p * 2 + tile, 64, blocks)

    for tile in range(4):
        for d in range(3):
            weight = out_rows[d : d + 1, :]
            w_o[16 * d : 16 * d + 16, 128 * tile : 128 * tile + 128] = jnp.where(
                iota((16, 128), 0) == lane // 32 + 4 * tile, weight, 0.0
            ).astype(BF16)

    for u in range(2):
        for slot in range(2):
            tall[slot, u, 0:8, :] = jnp.zeros((8, 640), F32)
            tall[slot, u, 136:144, :] = jnp.zeros((8, 640), F32)

    def marks_at(step):
        marks = []
        for u in range(2):
            z = 2 * step + u
            zone = 0 if z == 0 else (2 if z == nz + 1 else 1)
            marks.append([masks_ref[zone * 3 + k] for k in range(3)])
        return marks

    def embed(step):
        marks = marks_at(step)
        slot = step % 2
        shifted = []
        for u in range(2):
            z = 2 * step + u
            three = marks[u]

            def along(m):
                return jnp.concatenate(
                    [
                        jnp.where(lane < 64, m[0:1], m[1:2]),
                        jnp.where(lane < 64, m[2:3], m[3:4]),
                    ],
                    axis=1,
                )

            row = iota((32, 256), 0)
            mask = jnp.where(row < 4, along(three[0]), jnp.where(row < 20, along(three[1]), along(three[2])))
            masked = recv_ref[z].astype(F32) * mask
            column = iota((32, 256), 1)
            before = jnp.where(column == 0, 0.0, pltpu.roll(masked, 1, 1))
            after = jnp.where(column == 255, 0.0, pltpu.roll(masked, 255, 1))
            shifted += [before, masked, after, jnp.zeros((32, 256), F32)]
        shifted = jnp.concatenate(shifted, axis=0).astype(BF16)
        turned = lax.dot_general(perm_out[...], shifted, NT, preferred_element_type=F32).astype(BF16)
        for u in range(2):
            embedded = jnp.maximum(dot(turned[:, 128 * u : 128 * u + 128], w_e[...]), 0.0)
            even, odd = embedded[:128], embedded[128:]
            j = iota((128, 768), 0)
            planes[slot, u, 0:128] = jnp.where(j == 0, 0.0, pltpu.roll(odd, 1, 0)).astype(BF16)
            planes[slot, u, 128:256] = even.astype(BF16)
            planes[slot, u, 256:384] = odd.astype(BF16)
            planes[slot, u, 384:512] = jnp.where(j == 127, 0.0, pltpu.roll(even, 127, 0)).astype(BF16)

    def convolve(step):
        marks = marks_at(step)
        slot = step % 2

        def windows(tiles):
            return jnp.concatenate(
                [
                    jnp.concatenate(
                        [planes[slot, u, 128 * k : 128 * k + 128, 128 * t : 128 * t + 256] for k in range(4)],
                        axis=1,
                    )
                    for u in range(2)
                    for t in tiles
                ],
                axis=0,
            )

        def keep(summed, tiles, rows_of):
            for u in range(2):
                z = 2 * step + u
                for at, t in enumerate(tiles):
                    for p in range(2):
                        for y in range(4):
                            row = (u * len(tiles) + at) * 128 + 32 * y
                            piece = summed[row : row + 32, 128 * p : 128 * p + 128]
                            piece = jnp.maximum(piece, 0.0) * rows_of(marks[u], y)
                            feats[
                                z, 128 * p + 32 * y : 128 * p + 32 * y + 32, 128 * t : 128 * t + 128
                            ] = piece.astype(BF16)

        def inner(three, y):
            return three[1][y : y + 1]

        def outer(three, y):
            return jnp.where(lane < 64, three[0][y : y + 1], three[2][y : y + 1])

        keep(dot(windows(range(4)), w_c[...]), range(4), inner)
        keep(dot(windows([4]), w_h[...]), [4], outer)

    def lower(step):
        marks = marks_at(step)
        slot = step % 2

        def pairs(spans):
            return jnp.concatenate(
                [
                    jnp.concatenate(
                        [
                            feats[2 * step + u, 128 * p : 128 * p + 128, low:high]
                            for p in range(2)
                            for low, high in spans
                        ],
                        axis=1,
                    )
                    for u in range(2)
                ],
                axis=0,
            )

        lowered = [
            dot(pairs([(0, 256), (512, 640)]), w_d0[...]),
            dot(pairs([(128, 512)]), w_d1[...]),
            dot(pairs([(384, 640)]), w_d2[...]),
        ]
        for u in range(2):
            left, middle, right = marks[u]
            for y in range(4):
                m = middle[y : y + 1]
                rows_of = [
                    jnp.concatenate([jnp.where(lane < 64, left[y : y + 1], m), m], axis=1),
                    jnp.concatenate([m, m], axis=1),
                    jnp.where(lane < 64, m, right[y : y + 1]),
                ]
                for part, width in ((0, 256), (1, 256), (2, 128)):
                    piece = lowered[part][128 * u + 32 * y : 128 * u + 32 * y + 32]
                    piece = jnp.maximum(piece, 0.0) * rows_of[part]
                    tall[slot, u, 8 + 32 * y : 40 + 32 * y, 256 * part : 256 * part + width] = piece
            for b in range(3):
                downs[2 * step + u, b] = tall[slot, u, 7 + b : 135 + b, :].astype(BF16)

    steps = (nz + 2) // 2
    for at in range(steps + 2):
        if at < steps:
            embed(at)
        if 0 <= at - 1 < steps:
            convolve(at - 1)
        if at >= 2:
            lower(at - 2)

    def deepen(step):
        middle = masks_ref[4]
        rows_of = [jnp.concatenate([middle[y : y + 1]] * 2, axis=1) for y in range(4)]
        gathered = jnp.concatenate(
            [
                jnp.concatenate(
                    [
                        downs[4 * step + 2 * v + k, b, :, 128 * t : 128 * t + 256]
                        for k in range(4)
                        for b in range(3)
                    ],
                    axis=1,
                )
                for v in range(2)
                for t in range(4)
            ],
            axis=0,
        )
        deep_sum = dot(gathered, w_z[...])
        deep = jnp.concatenate(
            [
                jnp.maximum(deep_sum[32 * r : 32 * r + 32], 0.0) * rows_of[r % 4]
                for r in range(32)
            ],
            axis=0,
        ).astype(BF16)
        deep = jnp.concatenate(
            [
                jnp.concatenate(
                    [
                        deep[
                            (4 * v + 2 * g + h) * 128 : (4 * v + 2 * g + h) * 128 + 128,
                            128 * w : 128 * w + 128,
                        ]
                        for h in range(2)
                    ],
                    axis=1,
                )
                for g in range(2)
                for v in range(2)
                for w in range(2)
            ],
            axis=0,
        )
        return deep

    def decode(step, deep):
        middle = masks_ref[4]
        rows_of = [jnp.concatenate([middle[y : y + 1]] * 2, axis=1) for y in range(4)]
        raised = dot(deep, w_u[...])
        for g in range(2):
            for u in range(4):
                for p in range(2):
                    for y in range(4):
                        at = 128 * p + 32 * y
                        row = 512 * g + 128 * u + 32 * y
                        piece = raised[row : row + 32, 256 * p : 256 * p + 256]
                        skip = feats[4 * step + u + 1, at : at + 32, 256 * g : 256 * g + 256]
                        piece = jnp.maximum(piece + skip.astype(F32), 0.0) * rows_of[y]
                        decoded[step, u, at : at + 32, 256 * g : 256 * g + 256] = piece.astype(BF16)
        halves = []
        for u in range(4):
            projected = lax.dot_general(w_o[...], decoded[step, u], NT, preferred_element_type=F32)
            high = projected.astype(BF16)
            halves += [high, (projected - high.astype(F32)).astype(BF16)]
        ordered = dot(jnp.concatenate(halves, axis=0), perm_out[...])
        y_mask = jnp.concatenate(
            [
                jnp.where(lane < 64, middle[0:1], middle[1:2]),
                jnp.where(lane < 64, middle[2:3], middle[3:4]),
            ],
            axis=1,
        )
        for u in range(4):
            both = (ordered[96 * u : 96 * u + 48] + ordered[96 * u + 48 : 96 * u + 96]) * y_mask
            for d in range(3):
                logits_ref[d, 4 * step + u] = both[16 * d : 16 * d + 16]

    last = None
    for step in range(nz // 4):
        deep = deepen(step)
        if last is not None:
            decode(step - 1, last)
        last = deep
    decode(nz // 4 - 1, last)


def network(recv, masks, w_emb, w_one, w_down, w_deep, w_up, w_out, blk, nb, interpret=False):
    nz, length_y = nb, recv.shape[2]
    emb = jnp.transpose(w_emb, (1, 2, 0))
    one = jnp.transpose(w_one, (2, 3, 0, 1))
    down = jnp.transpose(w_down, (3, 2, 1, 0)).reshape(4, 32, 64)
    deep = jnp.transpose(w_deep, (2, 3, 4, 0, 1))
    up = jnp.transpose(w_up, (3, 2, 0, 1)).reshape(2, 64, 64)
    return pl.pallas_call(
        functools.partial(network_kernel, nb),
        out_shape=jax.ShapeDtypeStruct((3, nz, 16, length_y), F32),
        in_specs=[pl.BlockSpec(memory_space=pltpu.VMEM)] * 8
        + [pl.BlockSpec(memory_space=pltpu.SMEM)],
        out_specs=pl.BlockSpec(memory_space=pltpu.VMEM),
        scratch_shapes=[
            pltpu.VMEM((256, 256), BF16),
            pltpu.VMEM((128, 768), BF16),
            pltpu.VMEM((1024, 256), BF16),
            pltpu.VMEM((1024, 256), BF16),
            pltpu.VMEM((768, 256), BF16),
            pltpu.VMEM((768, 256), BF16),
            pltpu.VMEM((512, 128), BF16),
            pltpu.VMEM((3072, 256), BF16),
            pltpu.VMEM((256, 512), BF16),
            pltpu.VMEM((48, 512), BF16),
            pltpu.VMEM((27, 64, 128), F32),
            pltpu.VMEM((9, 32, 128), F32),
            pltpu.VMEM((4, 32, 128), F32),
            pltpu.VMEM((2, 2, 512, 768), BF16),
            pltpu.VMEM((nz + 2, 256, 640), BF16),
            pltpu.VMEM((2, 2, 144, 640), F32),
            pltpu.VMEM((nz + 2, 3, 128, 640), BF16),
            pltpu.VMEM((nz // 4, 4, 256, 512), BF16),
        ],
        compiler_params=pltpu.CompilerParams(vmem_limit_bytes=56 * 1024 * 1024),
        name="network",
        interpret=interpret,
    )(recv, masks, emb, one, down, deep, up, w_out, blk)


def solution(mesh):
    ns, nb = mesh.shape["sec"], mesh.shape["blk"]

    def per_device(raw, tissue, *weights):
        recv, masks = exchange(raw, tissue, ns, nb)
        blk = jnp.full((1,), lax.axis_index("blk"), jnp.int32)
        return network(recv, masks, *weights, blk, nb)

    placed = (P(("sec", "blk"), None, None), P("sec", "blk", None), P(), P(), P(), P(), P(), P())
    return jax.shard_map(
        per_device,
        mesh=mesh,
        in_specs=placed,
        out_specs=P(None, "sec", "blk", None),
        check_vma=False,
    )
```
